32 devices in a mesh: sub: 8 (over z, y), freq: 4 (over x, core).
Axes of the slice: x: 2, y: 2, z: 4, core: 2. Of those that a mesh axis runs over, the one named last changes fastest.
Arguments:
- freq_squared: float32 [16], P('freq'), may hold values from 0.05 to 1
- displacement: bfloat16 [1536, 2048], P('freq', 'sub'), may hold values from -6 to 6
- adjoint: bfloat16 [1536, 2048], P('freq', 'sub'), may hold values from -6 to 6
- incidence: int32 [24, 4], P('sub'), may hold values from 0 to 15, as said below
- block_count: int32 [24], P('sub'), may hold values from 1 to 4, as said below
- mode_count: int32 [24], P('sub'), may hold values from 1 to 128, as said below
- stiffness: bfloat16 [24, 512, 512], P('sub'), may hold values from -0.25 to 0.25
- mass_matrix: bfloat16 [24, 512, 512], P('sub'), may hold values from -0.25 to 0.25
- coupling: bfloat16 [24, 128, 512], P('sub'), may hold values from -0.25 to 0.25
- eigenvalues: float32 [24, 128], P('sub'), may hold values from 1.5 to 20
- flexibility: float32 [24, 512], P('sub'), may hold values from 0.2 to 1
Outputs:
- interface_residual: float32 [1536, 2048], P('freq', 'sub')
- eigen_gradient: float32 [24, 128], P('sub')
- coupling_gradient: float32 [24, 128, 512], P('sub', None, 'freq')
- flexibility_gradient: float32 [24, 512], P('sub')
The draws below stay inside these ranges and needn't reach their ends.
Inputs may be any that keep to these rules, and one draw needn't show every extreme that they name: `incidence`: every slot, live or not, names a block owned by the index of sub that holds the substructure or one at most 1 indices away (block b is owned by index b // 2). The first substructure of every index of sub touches, in live slots, a block of the owner 1 indices below and one 1 above wherever such owners exist. A substructure may name one block in several slots. `block_count`: the first substructure of every index of sub has 4 live slots. Modes j >= mode_count[s] are absent. The first substructure of every index of sub keeps 128 modes.
All inputs are finite; a program needn't handle non-finite values.
Results may differ from the reference program's by a relative error of at most 0.0029.
Values may be sent and summed in bfloat16 or wider, within the bound.
A program may use at most 64 MiB of HBM per device.

```python
import math
import jax
import jax.numpy as jnp
from jax import lax

B = 128
KMAX = 4
M = 128
F = 16
LC = 96
SUB_DEV = 3
BLK_DEV = 2
WIN = 1
KB = 512
S = 24
NB = 16


def draw_incidence(key, part):
    sub_ids = jnp.arange(S)
    device_ids = sub_ids // SUB_DEV
    first_key, second_key = jax.random.split(jax.random.fold_in(key, 11))
    shifts = jax.random.randint(first_key, (S, KMAX), -WIN, WIN + 1)
    slot_ids = jnp.arange(KMAX)[None, :]
    forced = jnp.where(slot_ids == 0, -WIN, jnp.where(slot_ids == 1, WIN, shifts))
    leading = (sub_ids % SUB_DEV == 0)[:, None]
    shifts = jnp.where(leading, forced, shifts)
    owners = jnp.clip(device_ids[:, None] + shifts, 0, NB // BLK_DEV - 1)
    local_block = jax.random.randint(second_key, (S, KMAX), 0, BLK_DEV)
    return (owners * BLK_DEV + local_block).astype(jnp.int32)


def draw_block_count(key, part):
    sub_ids = jnp.arange(S)
    counts = jax.random.randint(jax.random.fold_in(key, 23), (S,), 1, KMAX + 1)
    return jnp.where(sub_ids % SUB_DEV == 0, KMAX, counts).astype(jnp.int32)


def draw_mode_count(key, part):
    sub_ids = jnp.arange(S)
    counts = jax.random.randint(jax.random.fold_in(key, 37), (S,), M // 4, M + 1)
    return jnp.where(sub_ids % SUB_DEV == 0, M, counts).astype(jnp.int32)


def shard_levels(key, dims, shards, smallest, largest):
    gain = 1.0
    for dim, parts in shards:
        steps = jax.random.uniform(jax.random.fold_in(jax.random.fold_in(key, 6), dim), (parts,), jnp.float32, smallest / len(shards), largest / len(shards))
        gain = gain * jnp.repeat(jnp.exp(steps), dims[dim] // parts).reshape((-1,) + (1,) * (len(dims) - 1 - dim))
    return gain


def noise(rng, shape, deviation, most, cuts=(), dtype=jnp.bfloat16):
    level = shard_levels(rng, shape, cuts, -0.22, 0.18) if cuts else 1.0
    array = jax.random.normal(rng, shape, jnp.float32) * deviation * level
    return jnp.minimum(jnp.maximum(array, -most), most).astype(dtype)


def setup_inputs(seed: int = 0) -> dict:
    streams_of = jax.random.split(jax.random.key(seed), 12)
    freq_squared = jnp.clip(0.05 + 0.95 * jax.random.uniform(streams_of[0], (F,), jnp.float32) ** shard_levels(streams_of[0], (F,), ((0, 4),), -0.2, 0.2), 0.05, 1.0)
    displacement = noise(streams_of[1], (F * LC, NB * B), 1.0, 6.0, ((0, 4), (1, 8)))
    adjoint = noise(streams_of[2], (F * LC, NB * B), 1.0, 6.0, ((0, 4), (1, 8)))
    incidence = draw_incidence(jax.random.fold_in(streams_of[11], 71), 0)
    block_count = draw_block_count(jax.random.fold_in(streams_of[11], 71), 0)
    mode_count = draw_mode_count(jax.random.fold_in(streams_of[11], 71), 0)
    stiffness = noise(streams_of[6], (S, KB, KB), KB ** -0.5, 0.25, ((0, 8),))
    mass_matrix = noise(streams_of[7], (S, KB, KB), KB ** -0.5, 0.25, ((0, 8),))
    coupling = noise(streams_of[8], (S, M, KB), KB ** -0.5, 0.25, ((0, 8),))
    eigenvalues = jnp.clip(jnp.exp(math.log(20.0) - 2.5902672 * jax.random.uniform(streams_of[9], (S, M), jnp.float32) ** shard_levels(streams_of[9], (S, M), ((0, 8),), -0.2, 0.2)), 1.5, 20.0)
    flexibility = jnp.clip(0.2 + 0.8 * jax.random.uniform(streams_of[10], (S, KB), jnp.float32) ** shard_levels(streams_of[10], (S, KB), ((0, 8),), -0.2, 0.2), 0.2, 1.0)
    return dict(freq_squared=freq_squared, displacement=displacement, adjoint=adjoint, incidence=incidence, block_count=block_count, mode_count=mode_count, stiffness=stiffness, mass_matrix=mass_matrix, coupling=coupling, eigenvalues=eigenvalues, flexibility=flexibility)


def reference(freq_squared, displacement, adjoint, incidence, block_count, mode_count, stiffness, mass_matrix, coupling, eigenvalues, flexibility):
    columns = displacement.shape[0]
    squares = jnp.repeat(freq_squared, LC)
    fourth = squares * squares
    adjoint_blocks = adjoint.reshape(columns, NB, B)
    displacement_blocks = displacement.reshape(columns, NB, B)
    slot_range = jnp.arange(KMAX)
    mode_range = jnp.arange(M)

    def one_substructure(summed, per_sub):
        blocks, live_count, mode_total, stiff_sub, mass_sub, couple_sub, eigen_sub, flex_sub = per_sub
        live_slot = slot_range < live_count
        slot_mask = live_slot.astype(jnp.bfloat16)[None, :, None]
        adjoint_sub = (jnp.take(adjoint_blocks, blocks, axis=1) * slot_mask).reshape(columns, KB)
        displacement_sub = (jnp.take(displacement_blocks, blocks, axis=1) * slot_mask).reshape(columns, KB)
        modal_adjoint = jnp.dot(adjoint_sub, couple_sub.T, preferred_element_type=jnp.float32)
        modal_displacement = jnp.dot(displacement_sub, couple_sub.T, preferred_element_type=jnp.float32)
        inverse = 1.0 / (eigen_sub[None, :] - squares[:, None])
        factor = jnp.where(mode_range[None, :] < mode_total, fourth[:, None] * inverse, jnp.float32(0.0))
        weight_adjoint = (factor * modal_adjoint).astype(jnp.bfloat16)
        weight_displacement = (factor * modal_displacement).astype(jnp.bfloat16)
        eigen_part = jnp.sum(factor * inverse * modal_adjoint * modal_displacement, axis=0)
        flex_part = -jnp.sum(fourth[:, None] * adjoint_sub.astype(jnp.float32) * displacement_sub.astype(jnp.float32), axis=0)
        couple_part = -(jnp.dot(weight_adjoint.T, displacement_sub, preferred_element_type=jnp.float32)
                        + jnp.dot(weight_displacement.T, adjoint_sub, preferred_element_type=jnp.float32))
        response = (jnp.dot(adjoint_sub, stiff_sub.T, preferred_element_type=jnp.float32)
                    - squares[:, None] * jnp.dot(adjoint_sub, mass_sub.T, preferred_element_type=jnp.float32)
                    - jnp.dot(weight_adjoint, couple_sub, preferred_element_type=jnp.float32)
                    - fourth[:, None] * flex_sub[None, :] * adjoint_sub.astype(jnp.float32))
        for slot_index in range(KMAX):
            first_col = (blocks[slot_index] * B).astype(jnp.int32)
            current = lax.dynamic_slice_in_dim(summed, first_col, B, 1)
            added = response[:, slot_index * B:(slot_index + 1) * B] * live_slot[slot_index].astype(jnp.float32)
            summed = lax.dynamic_update_slice_in_dim(summed, current + added, first_col, 1)
        return summed, (eigen_part, flex_part, couple_part)

    initial = jnp.zeros((columns, NB * B), jnp.float32)
    summed, outputs = lax.scan(one_substructure, initial, (incidence, block_count, mode_count, stiffness, mass_matrix, coupling, eigenvalues, flexibility))
    eigen_gradient, flexibility_gradient, coupling_gradient = outputs
    return summed, eigen_gradient, coupling_gradient, flexibility_gradient
```

```python
import functools

import jax
import jax.numpy as jnp
from jax import lax
from jax.experimental import pallas as pl
from jax.experimental.pallas import tpu as pltpu
from jax.sharding import PartitionSpec as P

MESH = pl.DeviceIdType.MESH
NT = (((1,), (1,)), ((), ()))
NN = (((1,), (0,)), ((), ()))
TN = (((0,), (0,)), ((), ()))


def dot(a, b, dims):
    return lax.dot_general(a, b, dims, preferred_element_type=jnp.float32)


def kernel(
    n_sub,
    n_freq,
    chunks,
    freq_ref,
    inc_ref,
    count_ref,
    mode_ref,
    eig_ref,
    flex_ref,
    adj_ref,
    dis_ref,
    stiff_hbm,
    mass_hbm,
    coup_hbm,
    out_ref,
    eig_out,
    cg_out_ref,
    flex_out,
    *scratch,
):
    windows = scratch[:chunks]
    (
        stiff,
        mass,
        coup,
        resp,
        weights,
        picked,
        near_acc,
        far_out,
        far_in,
        near_out,
        near_in,
        pack,
        grad,
        grad_out,
        grad_in,
        own_sem,
        weight_sem,
        near_send,
        near_recv,
        relay_send,
        relay_recv,
        far_send,
        far_recv,
        back_send,
        back_recv,
        pack_send,
        pack_recv,
        grad_send,
        grad_recv,
    ) = scratch[chunks:]
    sub_here, slots = inc_ref.shape
    columns, owned_cells = adj_ref.shape
    rows = columns // chunks
    kb = stiff.shape[1]
    block = kb // slots
    owned = owned_cells // block
    modes = coup.shape[1]
    part = kb // n_freq

    me = lax.axis_index("sub")
    fr = lax.axis_index("freq")
    odd = me % 2
    step = 2 - 4 * odd
    partner = me + 1 - 2 * odd
    target = me + step
    source = me - step
    has_target = (target >= 0) & (target < n_sub)
    has_source = (source >= 0) & (source < n_sub)
    target = jnp.clip(target, 0, n_sub - 1)
    source = jnp.clip(source, 0, n_sub - 1)

    weight_copies = [
        pltpu.make_async_copy(hbm, vmem, weight_sem.at[i])
        for i, (hbm, vmem) in enumerate(((coup_hbm, coup), (stiff_hbm, stiff), (mass_hbm, mass)))
    ]
    own_copies = [
        [
            pltpu.make_async_copy(
                ref.at[pl.ds(c * rows, rows), :], windows[c].at[0, t], own_sem.at[c, t]
            )
            for t, ref in enumerate((adj_ref, dis_ref))
        ]
        for c in range(chunks)
    ]

    def remote(src, dst, send, recv, sub, freq):
        return pltpu.make_async_remote_copy(
            src_ref=src,
            dst_ref=dst,
            send_sem=send,
            recv_sem=recv,
            device_id=(sub, freq),
            device_id_type=MESH,
        )

    near_copies = [
        [
            remote(
                ref.at[pl.ds(c * rows, rows), :],
                windows[c].at[1, t],
                near_send.at[c, t],
                near_recv.at[c, t],
                partner,
                fr,
            )
            for t, ref in enumerate((adj_ref, dis_ref))
        ]
        for c in range(chunks)
    ]
    relay_copies = [
        [
            remote(
                windows[c].at[1, t],
                windows[c].at[2, t],
                relay_send.at[c, t],
                relay_recv.at[c, t],
                target,
                fr,
            )
            for t in range(2)
        ]
        for c in range(chunks)
    ]
    far_copies = [
        remote(far_out.at[c], far_in.at[c], far_send.at[c], far_recv.at[c], source, fr)
        for c in range(chunks)
    ]
    back_copies = [
        remote(near_out.at[c], near_in.at[c], back_send.at[c], back_recv.at[c], partner, fr)
        for c in range(chunks)
    ]
    peers = [(fr + d) % n_freq for d in range(n_freq)]
    pack_copies = [
        remote(pack.at[0], pack.at[d], pack_send.at[d], pack_recv.at[d], me, peers[d])
        for d in range(1, n_freq)
    ]
    grad_copies = [
        [
            remote(
                grad_out.at[s, peers[d]],
                grad_in.at[s, d],
                grad_send.at[s, d],
                grad_recv.at[s, d],
                me,
                peers[d],
            )
            for d in range(1, n_freq)
        ]
        for s in range(sub_here)
    ]

    barrier = pltpu.get_barrier_semaphore()

    def greet(sub, freq):
        pl.semaphore_signal(barrier, inc=1, device_id=(sub, freq), device_id_type=MESH)

    greet(partner, fr)
    for d in range(1, n_freq):
        greet(me, peers[d])

    @pl.when(has_target)
    def _():
        greet(target, fr)

    @pl.when(has_source)
    def _():
        greet(source, fr)

    for copies in own_copies[:1]:
        for copy in copies:
            copy.start()
    for copy in weight_copies:
        copy.start()
    for copies in own_copies[1:]:
        for copy in copies:
            copy.start()

    @pl.when(jnp.logical_not(has_target))
    def _():
        far_in[...] = jnp.zeros_like(far_in)

    pack[0] = jnp.zeros(pack.shape[1:], pack.dtype)
    pl.semaphore_wait(
        barrier, n_freq + has_target.astype(jnp.int32) + has_source.astype(jnp.int32)
    )
    for copies in near_copies:
        for copy in copies:
            copy.start()

    def relay(c):
        for copy in near_copies[c]:
            copy.wait_recv()

        @pl.when(has_target)
        def _():
            for copy in relay_copies[c]:
                copy.start()

    owners = (me, partner, me - 1 + 2 * odd)

    def hits(s, k):
        live = k < count_ref[s]
        named = inc_ref[s, k]
        return [live & (named == owner * owned + inner) for owner in owners for inner in range(owned)]

    def compute(c):
        window = windows[c]
        for copy in own_copies[c]:
            copy.wait()

        @pl.when(has_source)
        def _():
            for copy in relay_copies[c]:
                copy.wait_recv()

        w2 = freq_ref[c]
        w4 = w2 * w2
        base = c * 2 * rows

        def one(s, carry):
            a_parts, d_parts = [], []
            zero = jnp.zeros((rows, block), jnp.bfloat16)
            for k in range(slots):
                a_part, d_part = zero, zero
                for w, hit in enumerate(hits(s, k)):
                    place, inner = w // owned, w % owned
                    lane = pl.ds(inner * block, block)
                    a_part = jnp.where(hit, window[place, 0, :, lane], a_part)
                    d_part = jnp.where(hit, window[place, 1, :, lane], d_part)
                a_parts.append(a_part)
                d_parts.append(d_part)
            a = jnp.concatenate(a_parts, axis=1)
            d = jnp.concatenate(d_parts, axis=1)
            af = a.astype(jnp.float32)
            df = d.astype(jnp.float32)
            picked[s, pl.ds(base, rows), :] = d
            picked[s, pl.ds(base + rows, rows), :] = a
            pack[0, s, 0:1, :] += -w4 * jnp.sum(af * df, axis=0, keepdims=True)
            couple = coup[s]
            ma = dot(a, couple, NT)
            md = dot(d, couple, NT)
            inverse = 1.0 / (eig_ref[pl.ds(s, 1), :] - w2)
            mode_index = lax.broadcasted_iota(jnp.int32, (1, modes), 1)
            factor = jnp.where(mode_index < mode_ref[s], w4 * inverse, 0.0)
            wa = (factor * ma).astype(jnp.bfloat16)
            wd = (factor * md).astype(jnp.bfloat16)
            weights[s, pl.ds(base, rows), :] = wa
            weights[s, pl.ds(base + rows, rows), :] = wd
            pack[0, s, 1:2, 0:modes] += (factor * inverse) * jnp.sum(
                ma * md, axis=0, keepdims=True
            )
            resp[s] = (
                dot(a, stiff[s], NT)
                - w2 * dot(a, mass[s], NT)
                - dot(wa, couple, NN)
                - (w4 * flex_ref[pl.ds(s, 1), :]) * af
            )
            return carry

        if c == 0:
            for copy in weight_copies:
                copy.wait()
        lax.fori_loop(0, sub_here, one, 0)

        places = [
            (s, k, [jnp.where(hit, 1.0, 0.0).astype(jnp.float32) for hit in hits(s, k)])
            for s in range(sub_here)
            for k in range(slots)
        ]
        here = pl.ds(c * rows, rows)
        for place in range(3):
            for inner in range(owned):
                total = None
                for s, k, gains in places:
                    term = gains[place * owned + inner] * resp[s, :, k * block : (k + 1) * block]
                    total = term if total is None else total + term
                lane = pl.ds(inner * block, block)
                if place == 0:
                    out_ref[here, lane] = total
                elif place == 1:
                    near_acc[c, :, lane] = total
                else:
                    far_out[c, :, lane] = total.astype(far_out.dtype)

        @pl.when(has_source)
        def _():
            far_copies[c].start()

    def combine(c):
        @pl.when(has_target)
        def _():
            far_copies[c].wait_recv()

        near_out[c] = (near_acc[c] + far_in[c].astype(jnp.float32)).astype(near_out.dtype)
        back_copies[c].start()

    def finish(c):
        back_copies[c].wait_recv()
        out_ref[pl.ds(c * rows, rows), :] += near_in[c].astype(jnp.float32)

    relay(0)
    for c in range(chunks):
        if c + 1 < chunks:
            relay(c + 1)
        compute(c)
        if c >= 1:
            combine(c - 1)
        if c >= 2:
            finish(c - 2)

    for copy in pack_copies:
        copy.start()

    for s in range(sub_here):
        value = -dot(weights[s], picked[s], TN)
        for j in range(n_freq):
            piece = value[:, j * part : (j + 1) * part]
            grad[s, j] = piece
            grad_out[s, j] = piece.astype(grad_out.dtype)
        for copy in grad_copies[s]:
            copy.start()
        if s == 0:
            combine(chunks - 1)
    if chunks >= 2:
        finish(chunks - 2)

    for copy in pack_copies:
        copy.wait_recv()
    total = None
    for i in range(n_freq):
        term = pack[(fr - i + n_freq) % n_freq]
        total = term if total is None else total + term
    for s in range(sub_here):
        flex_out[s : s + 1, :] = total[s, 0:1, :]
        eig_out[s : s + 1, :] = total[s, 1:2, 0:modes]
    finish(chunks - 1)
    for s in range(sub_here):
        value = grad[s, fr]
        for d in range(1, n_freq):
            grad_copies[s][d - 1].wait_recv()
            value = value + grad_in[s, d].astype(jnp.float32)
        cg_out_ref[s] = value

    for c in range(chunks):
        for copy in near_copies[c]:
            copy.wait_send()
        back_copies[c].wait_send()

    @pl.when(has_target)
    def _():
        for c in range(chunks):
            for copy in relay_copies[c]:
                copy.wait_send()

    @pl.when(has_source)
    def _():
        for c in range(chunks):
            far_copies[c].wait_send()

    for copy in pack_copies:
        copy.wait_send()
    for s in range(sub_here):
        for copy in grad_copies[s]:
            copy.wait_send()


def shards(
    n_sub,
    n_freq,
    freq_squared,
    displacement,
    adjoint,
    incidence,
    block_count,
    mode_count,
    stiffness,
    mass_matrix,
    coupling,
    eigenvalues,
    flexibility,
):
    sub_here = incidence.shape[0]
    columns, owned_cells = displacement.shape
    chunks = freq_squared.shape[0]
    rows = columns // chunks
    kb = stiffness.shape[1]
    modes = coupling.shape[1]
    part = kb // n_freq
    bf16, f32 = jnp.bfloat16, jnp.float32
    smem = pl.BlockSpec(memory_space=pltpu.SMEM)
    vmem = pl.BlockSpec(memory_space=pltpu.VMEM)
    anywhere = pl.BlockSpec(memory_space=pl.ANY)
    dma = pltpu.SemaphoreType.DMA
    slab = (chunks, rows, owned_cells)
    scratch = [pltpu.VMEM((3, 2, rows, owned_cells), bf16) for _ in range(chunks)] + [
        pltpu.VMEM(stiffness.shape, bf16),
        pltpu.VMEM(mass_matrix.shape, bf16),
        pltpu.VMEM(coupling.shape, bf16),
        pltpu.VMEM((sub_here, rows, kb), f32),
        pltpu.VMEM((sub_here, 2 * columns, modes), bf16),
        pltpu.VMEM((sub_here, 2 * columns, kb), bf16),
        pltpu.VMEM(slab, f32),
        pltpu.VMEM(slab, bf16),
        pltpu.VMEM(slab, bf16),
        pltpu.VMEM(slab, bf16),
        pltpu.VMEM(slab, bf16),
        pltpu.VMEM((n_freq, sub_here, 8, kb), f32),
        pltpu.VMEM((sub_here, n_freq, modes, part), f32),
        pltpu.VMEM((sub_here, n_freq, modes, part), bf16),
        pltpu.VMEM((sub_here, n_freq, modes, part), bf16),
        dma((chunks, 2)),
        dma((3,)),
        dma((chunks, 2)),
        dma((chunks, 2)),
        dma((chunks, 2)),
        dma((chunks, 2)),
        dma((chunks,)),
        dma((chunks,)),
        dma((chunks,)),
        dma((chunks,)),
        dma((n_freq,)),
        dma((n_freq,)),
        dma((sub_here, n_freq)),
        dma((sub_here, n_freq)),
    ]
    return pl.pallas_call(
        functools.partial(kernel, n_sub, n_freq, chunks),
        out_shape=(
            jax.ShapeDtypeStruct((columns, owned_cells), f32),
            jax.ShapeDtypeStruct((sub_here, modes), f32),
            jax.ShapeDtypeStruct((sub_here, modes, part), f32),
            jax.ShapeDtypeStruct((sub_here, kb), f32),
        ),
        in_specs=[smem] * 4 + [vmem] * 2 + [anywhere] * 5,
        out_specs=(vmem,) * 4,
        scratch_shapes=scratch,
        compiler_params=pltpu.CompilerParams(
            collective_id=0, has_side_effects=True, vmem_limit_bytes=48 * 1024 * 1024
        ),
    )(
        freq_squared,
        incidence,
        block_count,
        mode_count,
        eigenvalues,
        flexibility,
        adjoint,
        displacement,
        stiffness,
        mass_matrix,
        coupling,
    )


def solution(mesh):
    in_specs = (
        P("freq"),
        P("freq", "sub"),
        P("freq", "sub"),
        P("sub", None),
        P("sub"),
        P("sub"),
        P("sub", None, None),
        P("sub", None, None),
        P("sub", None, None),
        P("sub", None),
        P("sub", None),
    )
    out_specs = (P("freq", "sub"), P("sub", None), P("sub", None, "freq"), P("sub", None))
    body = functools.partial(shards, mesh.shape["sub"], mesh.shape["freq"])
    return jax.shard_map(body, mesh=mesh, in_specs=in_specs, out_specs=out_specs, check_vma=False)
```

```python
import functools

import jax
import jax.numpy as jnp
from jax import lax
from jax.experimental import pallas as pl
from jax.experimental.pallas import tpu as pltpu
from jax.sharding import PartitionSpec as P

MESH = pl.DeviceIdType.MESH
NT = (((1,), (1,)), ((), ()))
NN = (((1,), (0,)), ((), ()))
TN = (((0,), (0,)), ((), ()))


def dot(a, b, dims):
    return lax.dot_general(a, b, dims, preferred_element_type=jnp.float32)


def kernel(
    n_sub,
    n_freq,
    chunks,
    freq_hbm,
    inc_hbm,
    count_hbm,
    mode_hbm,
    eig_hbm,
    flex_hbm,
    adj_ref,
    dis_ref,
    stiff_hbm,
    mass_hbm,
    coup_hbm,
    out_ref,
    eig_out,
    cg_out_ref,
    flex_out,
    *scratch,
):
    windows = scratch[:chunks]
    (
        freq_ref,
        inc_ref,
        count_ref,
        mode_ref,
        eig_ref,
        flex_ref,
        stiff,
        mass,
        coup,
        resp,
        weights,
        picked,
        near_acc,
        far_out,
        far_in,
        near_out,
        near_in,
        pack,
        grad,
        grad_out,
        grad_in,
        own_sem,
        weight_sem,
        small_sem,
        near_send,
        near_recv,
        relay_send,
        relay_recv,
        far_send,
        far_recv,
        back_send,
        back_recv,
        pack_send,
        pack_recv,
        grad_send,
        grad_recv,
    ) = scratch[chunks:]
    sub_here, slots = inc_ref.shape
    columns, owned_cells = adj_ref.shape
    rows = columns // chunks
    kb = stiff.shape[1]
    block = kb // slots
    owned = owned_cells // block
    modes = coup.shape[1]
    part = kb // n_freq

    me = lax.axis_index("sub")
    fr = lax.axis_index("freq")
    odd = me % 2
    step = 2 - 4 * odd
    partner = me + 1 - 2 * odd
    target = me + step
    source = me - step
    has_target = (target >= 0) & (target < n_sub)
    has_source = (source >= 0) & (source < n_sub)
    target = jnp.clip(target, 0, n_sub - 1)
    source = jnp.clip(source, 0, n_sub - 1)

    weight_copies = [
        pltpu.make_async_copy(hbm, vmem, weight_sem.at[i])
        for i, (hbm, vmem) in enumerate(((coup_hbm, coup), (stiff_hbm, stiff), (mass_hbm, mass)))
    ]
    small_copies = [
        pltpu.make_async_copy(hbm, local, small_sem.at[i])
        for i, (hbm, local) in enumerate(
            (
                (freq_hbm, freq_ref),
                (inc_hbm, inc_ref),
                (count_hbm, count_ref),
                (mode_hbm, mode_ref),
                (eig_hbm, eig_ref),
                (flex_hbm, flex_ref),
            )
        )
    ]
    own_copies = [
        [
            pltpu.make_async_copy(
                ref.at[pl.ds(c * rows, rows), :], windows[c].at[0, t], own_sem.at[c, t]
            )
            for t, ref in enumerate((adj_ref, dis_ref))
        ]
        for c in range(chunks)
    ]

    def remote(src, dst, send, recv, sub, freq):
        return pltpu.make_async_remote_copy(
            src_ref=src,
            dst_ref=dst,
            send_sem=send,
            recv_sem=recv,
            device_id=(sub, freq),
            device_id_type=MESH,
        )

    near_copies = [
        [
            remote(
                ref.at[pl.ds(c * rows, rows), :],
                windows[c].at[1, t],
                near_send.at[c, t],
                near_recv.at[c, t],
                partner,
                fr,
            )
            for t, ref in enumerate((adj_ref, dis_ref))
        ]
        for c in range(chunks)
    ]
    relay_copies = [
        [
            remote(
                windows[c].at[1, t],
                windows[c].at[2, t],
                relay_send.at[c, t],
                relay_recv.at[c, t],
                target,
                fr,
            )
            for t in range(2)
        ]
        for c in range(chunks)
    ]
    far_copies = [
        remote(far_out.at[c], far_in.at[c], far_send.at[c], far_recv.at[c], source, fr)
        for c in range(chunks)
    ]
    back_copies = [
        remote(near_out.at[c], near_in.at[c], back_send.at[c], back_recv.at[c], partner, fr)
        for c in range(chunks)
    ]
    peers = [(fr + d) % n_freq for d in range(n_freq)]
    pack_copies = [
        remote(pack.at[0], pack.at[d], pack_send.at[d], pack_recv.at[d], me, peers[d])
        for d in range(1, n_freq)
    ]
    grad_copies = [
        [
            remote(
                grad_out.at[s, peers[d]],
                grad_in.at[s, d],
                grad_send.at[s, d],
                grad_recv.at[s, d],
                me,
                peers[d],
            )
            for d in range(1, n_freq)
        ]
        for s in range(sub_here)
    ]

    barrier = pltpu.get_barrier_semaphore()

    def greet(sub, freq):
        pl.semaphore_signal(barrier, inc=1, device_id=(sub, freq), device_id_type=MESH)

    greet(partner, fr)
    for d in range(1, n_freq):
        greet(me, peers[d])

    @pl.when(has_target)
    def _():
        greet(target, fr)

    @pl.when(has_source)
    def _():
        greet(source, fr)

    for copy in small_copies:
        copy.start()
    for copies in own_copies[:1]:
        for copy in copies:
            copy.start()
    for copy in weight_copies:
        copy.start()
    for copies in own_copies[1:]:
        for copy in copies:
            copy.start()

    @pl.when(jnp.logical_not(has_target))
    def _():
        far_in[...] = jnp.zeros_like(far_in)

    pack[0] = jnp.zeros(pack.shape[1:], pack.dtype)
    pl.semaphore_wait(
        barrier, n_freq + has_target.astype(jnp.int32) + has_source.astype(jnp.int32)
    )
    for copies in near_copies:
        for copy in copies:
            copy.start()

    def relay(c):
        for copy in near_copies[c]:
            copy.wait_recv()

        @pl.when(has_target)
        def _():
            for copy in relay_copies[c]:
                copy.start()

    owners = (me, partner, me - 1 + 2 * odd)

    def hits(s, k):
        live = k < count_ref[s]
        named = inc_ref[s, k]
        return [live & (named == owner * owned + inner) for owner in owners for inner in range(owned)]

    def compute(c):
        window = windows[c]
        for copy in own_copies[c]:
            copy.wait()

        @pl.when(has_source)
        def _():
            for copy in relay_copies[c]:
                copy.wait_recv()

        if c == 0:
            for copy in small_copies + weight_copies:
                copy.wait()
        w2 = freq_ref[c]
        w4 = w2 * w2
        base = c * 2 * rows

        def one(s, carry):
            a_parts, d_parts = [], []
            zero = jnp.zeros((rows, block), jnp.bfloat16)
            for k in range(slots):
                a_part, d_part = zero, zero
                for w, hit in enumerate(hits(s, k)):
                    place, inner = w // owned, w % owned
                    lane = pl.ds(inner * block, block)
                    a_part = jnp.where(hit, window[place, 0, :, lane], a_part)
                    d_part = jnp.where(hit, window[place, 1, :, lane], d_part)
                a_parts.append(a_part)
                d_parts.append(d_part)
            a = jnp.concatenate(a_parts, axis=1)
            d = jnp.concatenate(d_parts, axis=1)
            af = a.astype(jnp.float32)
            df = d.astype(jnp.float32)
            picked[s, pl.ds(base, rows), :] = d
            picked[s, pl.ds(base + rows, rows), :] = a
            pack[0, s, 0:1, :] += -w4 * jnp.sum(af * df, axis=0, keepdims=True)
            couple = coup[s]
            ma = dot(a, couple, NT)
            md = dot(d, couple, NT)
            inverse = 1.0 / (eig_ref[pl.ds(s, 1), :] - w2)
            mode_index = lax.broadcasted_iota(jnp.int32, (1, modes), 1)
            factor = jnp.where(mode_index < mode_ref[s], w4 * inverse, 0.0)
            wa = (factor * ma).astype(jnp.bfloat16)
            wd = (factor * md).astype(jnp.bfloat16)
            weights[s, pl.ds(base, rows), :] = wa
            weights[s, pl.ds(base + rows, rows), :] = wd
            pack[0, s, 1:2, 0:modes] += (factor * inverse) * jnp.sum(
                ma * md, axis=0, keepdims=True
            )
            resp[s] = (
                dot(a, stiff[s], NT)
                - w2 * dot(a, mass[s], NT)
                - dot(wa, couple, NN)
                - (w4 * flex_ref[pl.ds(s, 1), :]) * af
            )
            return carry

        lax.fori_loop(0, sub_here, one, 0)

        places = [
            (s, k, [jnp.where(hit, 1.0, 0.0).astype(jnp.float32) for hit in hits(s, k)])
            for s in range(sub_here)
            for k in range(slots)
        ]
        here = pl.ds(c * rows, rows)
        for place in range(3):
            for inner in range(owned):
                total = None
                for s, k, gains in places:
                    term = gains[place * owned + inner] * resp[s, :, k * block : (k + 1) * block]
                    total = term if total is None else total + term
                lane = pl.ds(inner * block, block)
                if place == 0:
                    out_ref[here, lane] = total
                elif place == 1:
                    near_acc[c, :, lane] = total
                else:
                    far_out[c, :, lane] = total.astype(far_out.dtype)

        @pl.when(has_source)
        def _():
            far_copies[c].start()

    def combine(c):
        @pl.when(has_target)
        def _():
            far_copies[c].wait_recv()

        near_out[c] = (near_acc[c] + far_in[c].astype(jnp.float32)).astype(near_out.dtype)
        back_copies[c].start()

    def finish(c):
        back_copies[c].wait_recv()
        out_ref[pl.ds(c * rows, rows), :] += near_in[c].astype(jnp.float32)

    relay(0)
    for c in range(chunks):
        if c + 1 < chunks:
            relay(c + 1)
        compute(c)
        if c >= 1:
            combine(c - 1)
        if c >= 2:
            finish(c - 2)

    for copy in pack_copies:
        copy.start()

    for s in range(sub_here):
        value = -dot(weights[s], picked[s], TN)
        for j in range(n_freq):
            piece = value[:, j * part : (j + 1) * part]
            grad[s, j] = piece
            grad_out[s, j] = piece.astype(grad_out.dtype)
        for copy in grad_copies[s]:
            copy.start()
        if s == 0:
            combine(chunks - 1)
    if chunks >= 2:
        finish(chunks - 2)

    for copy in pack_copies:
        copy.wait_recv()
    total = None
    for i in range(n_freq):
        term = pack[(fr - i + n_freq) % n_freq]
        total = term if total is None else total + term
    for s in range(sub_here):
        flex_out[s : s + 1, :] = total[s, 0:1, :]
        eig_out[s : s + 1, :] = total[s, 1:2, 0:modes]
    finish(chunks - 1)
    for s in range(sub_here):
        value = grad[s, fr]
        for d in range(1, n_freq):
            grad_copies[s][d - 1].wait_recv()
            value = value + grad_in[s, d].astype(jnp.float32)
        cg_out_ref[s] = value

    for c in range(chunks):
        for copy in near_copies[c]:
            copy.wait_send()
        back_copies[c].wait_send()

    @pl.when(has_target)
    def _():
        for c in range(chunks):
            for copy in relay_copies[c]:
                copy.wait_send()

    @pl.when(has_source)
    def _():
        for c in range(chunks):
            far_copies[c].wait_send()

    for copy in pack_copies:
        copy.wait_send()
    for s in range(sub_here):
        for copy in grad_copies[s]:
            copy.wait_send()


def shards(
    n_sub,
    n_freq,
    freq_squared,
    displacement,
    adjoint,
    incidence,
    block_count,
    mode_count,
    stiffness,
    mass_matrix,
    coupling,
    eigenvalues,
    flexibility,
):
    sub_here = incidence.shape[0]
    columns, owned_cells = displacement.shape
    chunks = freq_squared.shape[0]
    rows = columns // chunks
    kb = stiffness.shape[1]
    modes = coupling.shape[1]
    part = kb // n_freq
    bf16, f32 = jnp.bfloat16, jnp.float32
    vmem = pl.BlockSpec(memory_space=pltpu.VMEM)
    hbm = pl.BlockSpec(memory_space=pltpu.HBM)
    dma = pltpu.SemaphoreType.DMA
    slab = (chunks, rows, owned_cells)
    scratch = [pltpu.VMEM((3, 2, rows, owned_cells), bf16) for _ in range(chunks)] + [
        pltpu.SMEM(freq_squared.shape, f32),
        pltpu.SMEM(incidence.shape, jnp.int32),
        pltpu.SMEM(block_count.shape, jnp.int32),
        pltpu.SMEM(mode_count.shape, jnp.int32),
        pltpu.VMEM(eigenvalues.shape, f32),
        pltpu.VMEM(flexibility.shape, f32),
        pltpu.VMEM(stiffness.shape, bf16),
        pltpu.VMEM(mass_matrix.shape, bf16),
        pltpu.VMEM(coupling.shape, bf16),
        pltpu.VMEM((sub_here, rows, kb), f32),
        pltpu.VMEM((sub_here, 2 * columns, modes), bf16),
        pltpu.VMEM((sub_here, 2 * columns, kb), bf16),
        pltpu.VMEM(slab, f32),
        pltpu.VMEM(slab, bf16),
        pltpu.VMEM(slab, bf16),
        pltpu.VMEM(slab, bf16),
        pltpu.VMEM(slab, bf16),
        pltpu.VMEM((n_freq, sub_here, 8, kb), f32),
        pltpu.VMEM((sub_here, n_freq, modes, part), f32),
        pltpu.VMEM((sub_here, n_freq, modes, part), bf16),
        pltpu.VMEM((sub_here, n_freq, modes, part), bf16),
        dma((chunks, 2)),
        dma((3,)),
        dma((6,)),
        dma((chunks, 2)),
        dma((chunks, 2)),
        dma((chunks, 2)),
        dma((chunks, 2)),
        dma((chunks,)),
        dma((chunks,)),
        dma((chunks,)),
        dma((chunks,)),
        dma((n_freq,)),
        dma((n_freq,)),
        dma((sub_here, n_freq)),
        dma((sub_here, n_freq)),
    ]
    return pl.pallas_call(
        functools.partial(kernel, n_sub, n_freq, chunks),
        out_shape=(
            jax.ShapeDtypeStruct((columns, owned_cells), f32),
            jax.ShapeDtypeStruct((sub_here, modes), f32),
            jax.ShapeDtypeStruct((sub_here, modes, part), f32),
            jax.ShapeDtypeStruct((sub_here, kb), f32),
        ),
        in_specs=[hbm] * 11,
        out_specs=(vmem,) * 4,
        scratch_shapes=scratch,
        compiler_params=pltpu.CompilerParams(
            collective_id=0, has_side_effects=True, vmem_limit_bytes=67043328
        ),
    )(
        freq_squared,
        incidence,
        block_count,
        mode_count,
        eigenvalues,
        flexibility,
        adjoint,
        displacement,
        stiffness,
        mass_matrix,
        coupling,
    )


def solution(mesh):
    in_specs = (
        P("freq"),
        P("freq", "sub"),
        P("freq", "sub"),
        P("sub", None),
        P("sub"),
        P("sub"),
        P("sub", None, None),
        P("sub", None, None),
        P("sub", None, None),
        P("sub", None),
        P("sub", None),
    )
    out_specs = (P("freq", "sub"), P("sub", None), P("sub", None, "freq"), P("sub", None))
    body = functools.partial(shards, mesh.shape["sub"], mesh.shape["freq"])
    return jax.shard_map(body, mesh=mesh, in_specs=in_specs, out_specs=out_specs, check_vma=False)
```

```python
import functools

import jax
import jax.numpy as jnp
from jax import lax
from jax.experimental import pallas as pl
from jax.experimental.pallas import tpu as pltpu
from jax.sharding import PartitionSpec as P

MESH = pl.DeviceIdType.MESH
NT = (((1,), (1,)), ((), ()))
NN = (((1,), (0,)), ((), ()))
TN = (((0,), (0,)), ((), ()))


def dot(a, b, dims):
    return lax.dot_general(a, b, dims, preferred_element_type=jnp.float32)


def kernel(
    n_sub,
    n_freq,
    chunks,
    freq_hbm,
    inc_hbm,
    count_hbm,
    mode_hbm,
    eig_hbm,
    flex_hbm,
    adj_ref,
    dis_ref,
    stiff_hbm,
    mass_hbm,
    coup_hbm,
    out_ref,
    eig_out,
    cg_out_ref,
    flex_out,
    *scratch,
):
    windows = scratch[:chunks]
    (
        freq_ref,
        inc_ref,
        count_ref,
        mode_ref,
        eig_ref,
        flex_ref,
        stiff,
        mass,
        coup,
        resp,
        weights,
        picked,
        near_acc,
        far_out,
        far_in,
        near_out,
        near_in,
        pack,
        grad,
        grad_out,
        grad_in,
        own_sem,
        weight_sem,
        small_sem,
        near_send,
        near_recv,
        relay_send,
        relay_recv,
        far_send,
        far_recv,
        back_send,
        back_recv,
        pack_send,
        pack_recv,
        grad_send,
        grad_recv,
    ) = scratch[chunks:]
    sub_here, slots = inc_ref.shape
    columns, owned_cells = adj_ref.shape
    rows = columns // chunks
    kb = stiff.shape[1]
    block = kb // slots
    owned = owned_cells // block
    modes = coup.shape[1]
    part = kb // n_freq

    me = lax.axis_index("sub")
    fr = lax.axis_index("freq")
    odd = me % 2
    step = 2 - 4 * odd
    partner = me + 1 - 2 * odd
    target = me + step
    source = me - step
    has_target = (target >= 0) & (target < n_sub)
    has_source = (source >= 0) & (source < n_sub)
    target = jnp.clip(target, 0, n_sub - 1)
    source = jnp.clip(source, 0, n_sub - 1)

    weight_copies = [
        pltpu.make_async_copy(hbm, vmem, weight_sem.at[i])
        for i, (hbm, vmem) in enumerate(((coup_hbm, coup), (stiff_hbm, stiff), (mass_hbm, mass)))
    ]
    small_copies = [
        pltpu.make_async_copy(hbm, local, small_sem.at[i])
        for i, (hbm, local) in enumerate(
            (
                (freq_hbm, freq_ref),
                (inc_hbm, inc_ref),
                (count_hbm, count_ref),
                (mode_hbm, mode_ref),
                (eig_hbm, eig_ref),
                (flex_hbm, flex_ref),
            )
        )
    ]
    own_copies = [
        [
            pltpu.make_async_copy(
                ref.at[pl.ds(c * rows, rows), :], windows[c].at[0, t], own_sem.at[c, t]
            )
            for t, ref in enumerate((adj_ref, dis_ref))
        ]
        for c in range(chunks)
    ]

    def remote(src, dst, send, recv, sub, freq):
        return pltpu.make_async_remote_copy(
            src_ref=src,
            dst_ref=dst,
            send_sem=send,
            recv_sem=recv,
            device_id=(sub, freq),
            device_id_type=MESH,
        )

    near_copies = [
        [
            remote(
                ref.at[pl.ds(c * rows, rows), :],
                windows[c].at[1, t],
                near_send.at[c, t],
                near_recv.at[c, t],
                partner,
                fr,
            )
            for t, ref in enumerate((adj_ref, dis_ref))
        ]
        for c in range(chunks)
    ]
    relay_copies = [
        [
            remote(
                windows[c].at[1, t],
                windows[c].at[2, t],
                relay_send.at[c, t],
                relay_recv.at[c, t],
                target,
                fr,
            )
            for t in range(2)
        ]
        for c in range(chunks)
    ]
    far_copies = [
        remote(far_out.at[c], far_in.at[c], far_send.at[c], far_recv.at[c], source, fr)
        for c in range(chunks)
    ]
    back_copies = [
        remote(near_out.at[c], near_in.at[c], back_send.at[c], back_recv.at[c], partner, fr)
        for c in range(chunks)
    ]
    peers = [(fr + d) % n_freq for d in range(n_freq)]
    pack_copies = [
        remote(pack.at[0], pack.at[d], pack_send.at[d], pack_recv.at[d], me, peers[d])
        for d in range(1, n_freq)
    ]
    grad_copies = [
        [
            remote(
                grad_out.at[s, peers[d]],
                grad_in.at[s, d],
                grad_send.at[s, d],
                grad_recv.at[s, d],
                me,
                peers[d],
            )
            for d in range(1, n_freq)
        ]
        for s in range(sub_here)
    ]

    barrier = pltpu.get_barrier_semaphore()

    def greet(sub, freq):
        pl.semaphore_signal(barrier, inc=1, device_id=(sub, freq), device_id_type=MESH)

    greet(partner, fr)
    for d in range(1, n_freq):
        greet(me, peers[d])

    @pl.when(has_target)
    def _():
        greet(target, fr)

    @pl.when(has_source)
    def _():
        greet(source, fr)

    for copy in small_copies:
        copy.start()
    for copies in own_copies[:1]:
        for copy in copies:
            copy.start()
    for copy in weight_copies:
        copy.start()
    for copies in own_copies[1:]:
        for copy in copies:
            copy.start()

    @pl.when(jnp.logical_not(has_target))
    def _():
        far_in[...] = jnp.zeros_like(far_in)

    pack[0] = jnp.zeros(pack.shape[1:], pack.dtype)
    pl.semaphore_wait(
        barrier, n_freq + has_target.astype(jnp.int32) + has_source.astype(jnp.int32)
    )
    for copies in near_copies:
        for copy in copies:
            copy.start()

    def relay(c):
        for copy in near_copies[c]:
            copy.wait_recv()

        @pl.when(has_target)
        def _():
            for copy in relay_copies[c]:
                copy.start()

    owners = (me, partner, me - 1 + 2 * odd)

    def hits(s, k):
        live = k < count_ref[s]
        named = inc_ref[s, k]
        return [live & (named == owner * owned + inner) for owner in owners for inner in range(owned)]

    def compute(c):
        window = windows[c]
        for copy in own_copies[c]:
            copy.wait()

        @pl.when(has_source)
        def _():
            for copy in relay_copies[c]:
                copy.wait_recv()

        if c == 0:
            for copy in small_copies + weight_copies:
                copy.wait()
        w2 = freq_ref[c]
        w4 = w2 * w2
        base = c * 2 * rows

        def one(s, carry):
            a_parts, d_parts = [], []
            zero = jnp.zeros((rows, block), jnp.bfloat16)
            for k in range(slots):
                a_part, d_part = zero, zero
                for w, hit in enumerate(hits(s, k)):
                    place, inner = w // owned, w % owned
                    lane = pl.ds(inner * block, block)
                    a_part = jnp.where(hit, window[place, 0, :, lane], a_part)
                    d_part = jnp.where(hit, window[place, 1, :, lane], d_part)
                a_parts.append(a_part)
                d_parts.append(d_part)
            a = jnp.concatenate(a_parts, axis=1)
            d = jnp.concatenate(d_parts, axis=1)
            af = a.astype(jnp.float32)
            df = d.astype(jnp.float32)
            picked[s, pl.ds(base, rows), :] = d
            picked[s, pl.ds(base + rows, rows), :] = a
            pack[0, s, 0:1, :] += -w4 * jnp.sum(af * df, axis=0, keepdims=True)
            couple = coup[s]
            ma = dot(a, couple, NT)
            md = dot(d, couple, NT)
            inverse = 1.0 / (eig_ref[pl.ds(s, 1), :] - w2)
            mode_index = lax.broadcasted_iota(jnp.int32, (1, modes), 1)
            factor = jnp.where(mode_index < mode_ref[s], w4 * inverse, 0.0)
            wa = (factor * ma).astype(jnp.bfloat16)
            wd = (factor * md).astype(jnp.bfloat16)
            weights[s, pl.ds(base, rows), :] = wa
            weights[s, pl.ds(base + rows, rows), :] = wd
            pack[0, s, 1:2, 0:modes] += (factor * inverse) * jnp.sum(
                ma * md, axis=0, keepdims=True
            )
            resp[s] = (
                dot(a, stiff[s], NT)
                - w2 * dot(a, mass[s], NT)
                - dot(wa, couple, NN)
                - (w4 * flex_ref[pl.ds(s, 1), :]) * af
            )
            return carry

        lax.fori_loop(0, sub_here, one, 0)

        places = [
            (s, k, [jnp.where(hit, 1.0, 0.0).astype(jnp.float32) for hit in hits(s, k)])
            for s in range(sub_here)
            for k in range(slots)
        ]
        here = pl.ds(c * rows, rows)
        for place in range(3):
            for inner in range(owned):
                total = None
                for s, k, gains in places:
                    term = gains[place * owned + inner] * resp[s, :, k * block : (k + 1) * block]
                    total = term if total is None else total + term
                lane = pl.ds(inner * block, block)
                if place == 0:
                    out_ref[here, lane] = total
                elif place == 1:
                    near_acc[c, :, lane] = total
                else:
                    far_out[c, :, lane] = total.astype(far_out.dtype)

        @pl.when(has_source)
        def _():
            far_copies[c].start()

    def combine(c):
        @pl.when(has_target)
        def _():
            far_copies[c].wait_recv()

        near_out[c] = (near_acc[c] + far_in[c].astype(jnp.float32)).astype(near_out.dtype)
        back_copies[c].start()

    def finish(c):
        back_copies[c].wait_recv()
        out_ref[pl.ds(c * rows, rows), :] += near_in[c].astype(jnp.float32)

    relay(0)
    for c in range(chunks):
        if c + 1 < chunks:
            relay(c + 1)
        compute(c)
        if c >= 1:
            combine(c - 1)
        if c >= 2:
            finish(c - 2)

    for copy in pack_copies:
        copy.start()

    for s in range(sub_here):
        value = -dot(weights[s], picked[s], TN)
        for j in range(n_freq):
            piece = value[:, j * part : (j + 1) * part]
            grad[s, j] = piece
            grad_out[s, j] = piece.astype(grad_out.dtype)
        for copy in grad_copies[s]:
            copy.start()
        if s == 0:
            combine(chunks - 1)
    if chunks >= 2:
        finish(chunks - 2)

    for copy in pack_copies:
        copy.wait_recv()
    total = None
    for i in range(n_freq):
        term = pack[(fr - i + n_freq) % n_freq]
        total = term if total is None else total + term
    for s in range(sub_here):
        flex_out[s : s + 1, :] = total[s, 0:1, :]
        eig_out[s : s + 1, :] = total[s, 1:2, 0:modes]
    finish(chunks - 1)
    for s in range(sub_here):
        value = grad[s, fr]
        for d in range(1, n_freq):
            grad_copies[s][d - 1].wait_recv()
            value = value + grad_in[s, d].astype(jnp.float32)
        cg_out_ref[s] = value

    for c in range(chunks):
        for copy in near_copies[c]:
            copy.wait_send()
        back_copies[c].wait_send()

    @pl.when(has_target)
    def _():
        for c in range(chunks):
            for copy in relay_copies[c]:
                copy.wait_send()

    @pl.when(has_source)
    def _():
        for c in range(chunks):
            far_copies[c].wait_send()

    for copy in pack_copies:
        copy.wait_send()
    for s in range(sub_here):
        for copy in grad_copies[s]:
            copy.wait_send()


def write_out(*refs):
    count = len(refs) // 2
    sems = refs[-1]
    copies = [
        pltpu.make_async_copy(refs[i], refs[count + i], sems.at[i]) for i in range(count)
    ]
    for copy in copies:
        copy.start()
    for copy in copies:
        copy.wait()


def shards(
    n_sub,
    n_freq,
    freq_squared,
    displacement,
    adjoint,
    incidence,
    block_count,
    mode_count,
    stiffness,
    mass_matrix,
    coupling,
    eigenvalues,
    flexibility,
):
    sub_here = incidence.shape[0]
    columns, owned_cells = displacement.shape
    chunks = freq_squared.shape[0]
    rows = columns // chunks
    kb = stiffness.shape[1]
    modes = coupling.shape[1]
    part = kb // n_freq
    bf16, f32 = jnp.bfloat16, jnp.float32
    vmem = pl.BlockSpec(memory_space=pltpu.VMEM)
    hbm = pl.BlockSpec(memory_space=pltpu.HBM)
    dma = pltpu.SemaphoreType.DMA
    slab = (chunks, rows, owned_cells)
    scratch = [pltpu.VMEM((3, 2, rows, owned_cells), bf16) for _ in range(chunks)] + [
        pltpu.SMEM(freq_squared.shape, f32),
        pltpu.SMEM(incidence.shape, jnp.int32),
        pltpu.SMEM(block_count.shape, jnp.int32),
        pltpu.SMEM(mode_count.shape, jnp.int32),
        pltpu.VMEM(eigenvalues.shape, f32),
        pltpu.VMEM(flexibility.shape, f32),
        pltpu.VMEM(stiffness.shape, bf16),
        pltpu.VMEM(mass_matrix.shape, bf16),
        pltpu.VMEM(coupling.shape, bf16),
        pltpu.VMEM((sub_here, rows, kb), f32),
        pltpu.VMEM((sub_here, 2 * columns, modes), bf16),
        pltpu.VMEM((sub_here, 2 * columns, kb), bf16),
        pltpu.VMEM(slab, f32),
        pltpu.VMEM(slab, bf16),
        pltpu.VMEM(slab, bf16),
        pltpu.VMEM(slab, bf16),
        pltpu.VMEM(slab, bf16),
        pltpu.VMEM((n_freq, sub_here, 8, kb), f32),
        pltpu.VMEM((sub_here, n_freq, modes, part), f32),
        pltpu.VMEM((sub_here, n_freq, modes, part), bf16),
        pltpu.VMEM((sub_here, n_freq, modes, part), bf16),
        dma((chunks, 2)),
        dma((3,)),
        dma((6,)),
        dma((chunks, 2)),
        dma((chunks, 2)),
        dma((chunks, 2)),
        dma((chunks, 2)),
        dma((chunks,)),
        dma((chunks,)),
        dma((chunks,)),
        dma((chunks,)),
        dma((n_freq,)),
        dma((n_freq,)),
        dma((sub_here, n_freq)),
        dma((sub_here, n_freq)),
    ]
    results = pl.pallas_call(
        functools.partial(kernel, n_sub, n_freq, chunks),
        out_shape=(
            jax.ShapeDtypeStruct((columns, owned_cells), f32),
            jax.ShapeDtypeStruct((sub_here, modes), f32),
            jax.ShapeDtypeStruct((sub_here, modes, part), f32),
            jax.ShapeDtypeStruct((sub_here, kb), f32),
        ),
        in_specs=[hbm] * 11,
        out_specs=(vmem,) * 4,
        scratch_shapes=scratch,
        compiler_params=pltpu.CompilerParams(
            collective_id=0, has_side_effects=True, vmem_limit_bytes=48 * 1024 * 1024
        ),
    )(
        *(
            pltpu.with_memory_space_constraint(x, pltpu.HBM)
            for x in (
                freq_squared,
                incidence,
                block_count,
                mode_count,
                eigenvalues,
                flexibility,
                adjoint,
                displacement,
                stiffness,
                mass_matrix,
                coupling,
            )
        )
    )
    return pl.pallas_call(
        write_out,
        out_shape=tuple(jax.ShapeDtypeStruct(x.shape, x.dtype) for x in results),
        in_specs=[vmem] * 4,
        out_specs=(pl.BlockSpec(memory_space=pltpu.HBM),) * 4,
        scratch_shapes=[dma((4,))],
        compiler_params=pltpu.CompilerParams(vmem_limit_bytes=4 * 1024 * 1024),
    )(*results)


def solution(mesh):
    in_specs = (
        P("freq"),
        P("freq", "sub"),
        P("freq", "sub"),
        P("sub", None),
        P("sub"),
        P("sub"),
        P("sub", None, None),
        P("sub", None, None),
        P("sub", None, None),
        P("sub", None),
        P("sub", None),
    )
    out_specs = (P("freq", "sub"), P("sub", None), P("sub", None, "freq"), P("sub", None))
    body = functools.partial(shards, mesh.shape["sub"], mesh.shape["freq"])
    return jax.shard_map(body, mesh=mesh, in_specs=in_specs, out_specs=out_specs, check_vma=False)
```

```python
import functools

import jax
import jax.numpy as jnp
from jax import lax
from jax.experimental import pallas as pl
from jax.experimental.pallas import tpu as pltpu
from jax.sharding import PartitionSpec as P

MESH = pl.DeviceIdType.MESH
NT = (((1,), (1,)), ((), ()))
NN = (((1,), (0,)), ((), ()))
TN = (((0,), (0,)), ((), ()))


def dot(a, b, dims):
    return lax.dot_general(a, b, dims, preferred_element_type=jnp.float32)


def kernel(
    n_sub,
    n_freq,
    chunks,
    freq_hbm,
    inc_hbm,
    count_hbm,
    mode_hbm,
    eig_hbm,
    flex_hbm,
    adj_ref,
    dis_ref,
    stiff_hbm,
    mass_hbm,
    coup_hbm,
    out_ref,
    eig_out,
    cg_out_ref,
    flex_out,
    *scratch,
):
    windows = scratch[:chunks]
    (
        freq_ref,
        inc_ref,
        count_ref,
        mode_ref,
        eig_ref,
        flex_ref,
        stiff,
        mass,
        coup,
        resp,
        weights,
        picked,
        near_acc,
        far_out,
        far_in,
        near_out,
        near_in,
        pack,
        grad,
        grad_out,
        grad_in,
        own_sem,
        weight_sem,
        small_sem,
        near_send,
        near_recv,
        relay_send,
        relay_recv,
        far_send,
        far_recv,
        back_send,
        back_recv,
        pack_send,
        pack_recv,
        grad_send,
        grad_recv,
    ) = scratch[chunks:]
    sub_here, slots = inc_ref.shape
    columns, owned_cells = adj_ref.shape
    rows = columns // chunks
    kb = stiff.shape[1]
    block = kb // slots
    owned = owned_cells // block
    modes = coup.shape[1]
    part = kb // n_freq

    me = lax.axis_index("sub")
    fr = lax.axis_index("freq")
    odd = me % 2
    step = 2 - 4 * odd
    partner = me + 1 - 2 * odd
    target = me + step
    source = me - step
    has_target = (target >= 0) & (target < n_sub)
    has_source = (source >= 0) & (source < n_sub)
    target = jnp.clip(target, 0, n_sub - 1)
    source = jnp.clip(source, 0, n_sub - 1)

    weight_copies = [
        pltpu.make_async_copy(hbm, vmem, weight_sem.at[i])
        for i, (hbm, vmem) in enumerate(((coup_hbm, coup), (stiff_hbm, stiff), (mass_hbm, mass)))
    ]
    small_copies = [
        pltpu.make_async_copy(hbm, local, small_sem.at[i])
        for i, (hbm, local) in enumerate(
            (
                (freq_hbm, freq_ref),
                (inc_hbm, inc_ref),
                (count_hbm, count_ref),
                (mode_hbm, mode_ref),
                (eig_hbm, eig_ref),
                (flex_hbm, flex_ref),
            )
        )
    ]
    own_copies = [
        [
            pltpu.make_async_copy(
                ref.at[pl.ds(c * rows, rows), :], windows[c].at[0, t], own_sem.at[c, t]
            )
            for t, ref in enumerate((adj_ref, dis_ref))
        ]
        for c in range(chunks)
    ]

    def remote(src, dst, send, recv, sub, freq):
        return pltpu.make_async_remote_copy(
            src_ref=src,
            dst_ref=dst,
            send_sem=send,
            recv_sem=recv,
            device_id=(sub, freq),
            device_id_type=MESH,
        )

    near_copies = [
        [
            remote(
                ref.at[pl.ds(c * rows, rows), :],
                windows[c].at[1, t],
                near_send.at[c, t],
                near_recv.at[c, t],
                partner,
                fr,
            )
            for t, ref in enumerate((adj_ref, dis_ref))
        ]
        for c in range(chunks)
    ]
    relay_copies = [
        [
            remote(
                windows[c].at[1, t],
                windows[c].at[2, t],
                relay_send.at[c, t],
                relay_recv.at[c, t],
                target,
                fr,
            )
            for t in range(2)
        ]
        for c in range(chunks)
    ]
    far_copies = [
        remote(far_out.at[c], far_in.at[c], far_send.at[c], far_recv.at[c], source, fr)
        for c in range(chunks)
    ]
    back_copies = [
        remote(near_out.at[c], near_in.at[c], back_send.at[c], back_recv.at[c], partner, fr)
        for c in range(chunks)
    ]
    peers = [(fr + d) % n_freq for d in range(n_freq)]
    pack_copies = [
        remote(pack.at[0], pack.at[d], pack_send.at[d], pack_recv.at[d], me, peers[d])
        for d in range(1, n_freq)
    ]
    grad_copies = [
        [
            remote(
                grad_out.at[s, peers[d]],
                grad_in.at[s, d],
                grad_send.at[s, d],
                grad_recv.at[s, d],
                me,
                peers[d],
            )
            for d in range(1, n_freq)
        ]
        for s in range(sub_here)
    ]

    barrier = pltpu.get_barrier_semaphore()

    def greet(sub, freq):
        pl.semaphore_signal(barrier, inc=1, device_id=(sub, freq), device_id_type=MESH)

    greet(partner, fr)
    for d in range(1, n_freq):
        greet(me, peers[d])

    @pl.when(has_target)
    def _():
        greet(target, fr)

    @pl.when(has_source)
    def _():
        greet(source, fr)

    for copy in small_copies:
        copy.start()
    for copies in own_copies[:1]:
        for copy in copies:
            copy.start()
    for copy in weight_copies:
        copy.start()
    for copies in own_copies[1:]:
        for copy in copies:
            copy.start()

    @pl.when(jnp.logical_not(has_target))
    def _():
        far_in[...] = jnp.zeros_like(far_in)

    pack[0] = jnp.zeros(pack.shape[1:], pack.dtype)
    pl.semaphore_wait(
        barrier, n_freq + has_target.astype(jnp.int32) + has_source.astype(jnp.int32)
    )
    for copies in near_copies:
        for copy in copies:
            copy.start()

    def relay(c):
        for copy in near_copies[c]:
            copy.wait_recv()

        @pl.when(has_target)
        def _():
            for copy in relay_copies[c]:
                copy.start()

    owners = (me, partner, me - 1 + 2 * odd)

    def hits(s, k):
        live = k < count_ref[s]
        named = inc_ref[s, k]
        return [live & (named == owner * owned + inner) for owner in owners for inner in range(owned)]

    def compute(c):
        window = windows[c]
        for copy in own_copies[c]:
            copy.wait()

        @pl.when(has_source)
        def _():
            for copy in relay_copies[c]:
                copy.wait_recv()

        if c == 0:
            for copy in small_copies + weight_copies:
                copy.wait()
        w2 = freq_ref[c]
        w4 = w2 * w2
        base = c * 2 * rows

        def one(s, carry):
            a_parts, d_parts = [], []
            zero = jnp.zeros((rows, block), jnp.bfloat16)
            for k in range(slots):
                a_part, d_part = zero, zero
                for w, hit in enumerate(hits(s, k)):
                    place, inner = w // owned, w % owned
                    lane = pl.ds(inner * block, block)
                    a_part = jnp.where(hit, window[place, 0, :, lane], a_part)
                    d_part = jnp.where(hit, window[place, 1, :, lane], d_part)
                a_parts.append(a_part)
                d_parts.append(d_part)
            a = jnp.concatenate(a_parts, axis=1)
            d = jnp.concatenate(d_parts, axis=1)
            af = a.astype(jnp.float32)
            df = d.astype(jnp.float32)
            picked[s, pl.ds(base, rows), :] = d
            picked[s, pl.ds(base + rows, rows), :] = a
            pack[0, s, 0:1, :] += -w4 * jnp.sum(af * df, axis=0, keepdims=True)
            couple = coup[s]
            ma = dot(a, couple, NT)
            md = dot(d, couple, NT)
            inverse = 1.0 / (eig_ref[pl.ds(s, 1), :] - w2)
            mode_index = lax.broadcasted_iota(jnp.int32, (1, modes), 1)
            factor = jnp.where(mode_index < mode_ref[s], w4 * inverse, 0.0)
            wa = (factor * ma).astype(jnp.bfloat16)
            wd = (factor * md).astype(jnp.bfloat16)
            weights[s, pl.ds(base, rows), :] = wa
            weights[s, pl.ds(base + rows, rows), :] = wd
            pack[0, s, 1:2, 0:modes] += (factor * inverse) * jnp.sum(
                ma * md, axis=0, keepdims=True
            )
            resp[s] = (
                dot(a, stiff[s], NT)
                - w2 * dot(a, mass[s], NT)
                - dot(wa, couple, NN)
                - (w4 * flex_ref[pl.ds(s, 1), :]) * af
            )
            return carry

        lax.fori_loop(0, sub_here, one, 0)

        places = [
            (s, k, [jnp.where(hit, 1.0, 0.0).astype(jnp.float32) for hit in hits(s, k)])
            for s in range(sub_here)
            for k in range(slots)
        ]
        here = pl.ds(c * rows, rows)
        for place in (2, 1, 0):
            for inner in range(owned):
                total = None
                for s, k, gains in places:
                    term = gains[place * owned + inner] * resp[s, :, k * block : (k + 1) * block]
                    total = term if total is None else total + term
                lane = pl.ds(inner * block, block)
                if place == 0:
                    out_ref[here, lane] = total
                elif place == 1:
                    near_acc[c, :, lane] = total
                else:
                    far_out[c, :, lane] = total.astype(far_out.dtype)

            if place == 2:

                @pl.when(has_source)
                def _():
                    far_copies[c].start()

    def combine(c):
        @pl.when(has_target)
        def _():
            far_copies[c].wait_recv()

        near_out[c] = (near_acc[c] + far_in[c].astype(jnp.float32)).astype(near_out.dtype)
        back_copies[c].start()

    def finish(c):
        back_copies[c].wait_recv()
        out_ref[pl.ds(c * rows, rows), :] += near_in[c].astype(jnp.float32)

    relay(0)
    for c in range(chunks):
        if c + 1 < chunks:
            relay(c + 1)
        compute(c)
        if c >= 2:
            combine(c - 2)

    for copy in pack_copies:
        copy.start()

    for s in range(sub_here):
        value = -dot(weights[s], picked[s], TN)
        for j in range(n_freq):
            piece = value[:, j * part : (j + 1) * part]
            grad[s, j] = piece
            grad_out[s, j] = piece.astype(grad_out.dtype)
        for copy in grad_copies[s]:
            copy.start()
    for c in range(max(chunks - 2, 0), chunks):
        combine(c)
    for c in range(chunks - 1):
        finish(c)

    for copy in pack_copies:
        copy.wait_recv()
    total = None
    for i in range(n_freq):
        term = pack[(fr - i + n_freq) % n_freq]
        total = term if total is None else total + term
    for s in range(sub_here):
        flex_out[s : s + 1, :] = total[s, 0:1, :]
        eig_out[s : s + 1, :] = total[s, 1:2, 0:modes]
    finish(chunks - 1)
    for s in range(sub_here):
        value = grad[s, fr]
        for d in range(1, n_freq):
            grad_copies[s][d - 1].wait_recv()
            value = value + grad_in[s, d].astype(jnp.float32)
        cg_out_ref[s] = value

    for c in range(chunks):
        for copy in near_copies[c]:
            copy.wait_send()
        back_copies[c].wait_send()

    @pl.when(has_target)
    def _():
        for c in range(chunks):
            for copy in relay_copies[c]:
                copy.wait_send()

    @pl.when(has_source)
    def _():
        for c in range(chunks):
            far_copies[c].wait_send()

    for copy in pack_copies:
        copy.wait_send()
    for s in range(sub_here):
        for copy in grad_copies[s]:
            copy.wait_send()


def write_out(*refs):
    count = len(refs) // 2
    sems = refs[-1]
    copies = [
        pltpu.make_async_copy(refs[i], refs[count + i], sems.at[i]) for i in range(count)
    ]
    for copy in copies:
        copy.start()
    for copy in copies:
        copy.wait()


def shards(
    n_sub,
    n_freq,
    freq_squared,
    displacement,
    adjoint,
    incidence,
    block_count,
    mode_count,
    stiffness,
    mass_matrix,
    coupling,
    eigenvalues,
    flexibility,
):
    sub_here = incidence.shape[0]
    columns, owned_cells = displacement.shape
    chunks = freq_squared.shape[0]
    rows = columns // chunks
    kb = stiffness.shape[1]
    modes = coupling.shape[1]
    part = kb // n_freq
    bf16, f32 = jnp.bfloat16, jnp.float32
    vmem = pl.BlockSpec(memory_space=pltpu.VMEM)
    hbm = pl.BlockSpec(memory_space=pltpu.HBM)
    dma = pltpu.SemaphoreType.DMA
    slab = (chunks, rows, owned_cells)
    scratch = [pltpu.VMEM((3, 2, rows, owned_cells), bf16) for _ in range(chunks)] + [
        pltpu.SMEM(freq_squared.shape, f32),
        pltpu.SMEM(incidence.shape, jnp.int32),
        pltpu.SMEM(block_count.shape, jnp.int32),
        pltpu.SMEM(mode_count.shape, jnp.int32),
        pltpu.VMEM(eigenvalues.shape, f32),
        pltpu.VMEM(flexibility.shape, f32),
        pltpu.VMEM(stiffness.shape, bf16),
        pltpu.VMEM(mass_matrix.shape, bf16),
        pltpu.VMEM(coupling.shape, bf16),
        pltpu.VMEM((sub_here, rows, kb), f32),
        pltpu.VMEM((sub_here, 2 * columns, modes), bf16),
        pltpu.VMEM((sub_here, 2 * columns, kb), bf16),
        pltpu.VMEM(slab, f32),
        pltpu.VMEM(slab, bf16),
        pltpu.VMEM(slab, bf16),
        pltpu.VMEM(slab, bf16),
        pltpu.VMEM(slab, bf16),
        pltpu.VMEM((n_freq, sub_here, 8, kb), f32),
        pltpu.VMEM((sub_here, n_freq, modes, part), f32),
        pltpu.VMEM((sub_here, n_freq, modes, part), bf16),
        pltpu.VMEM((sub_here, n_freq, modes, part), bf16),
        dma((chunks, 2)),
        dma((3,)),
        dma((6,)),
        dma((chunks, 2)),
        dma((chunks, 2)),
        dma((chunks, 2)),
        dma((chunks, 2)),
        dma((chunks,)),
        dma((chunks,)),
        dma((chunks,)),
        dma((chunks,)),
        dma((n_freq,)),
        dma((n_freq,)),
        dma((sub_here, n_freq)),
        dma((sub_here, n_freq)),
    ]
    results = pl.pallas_call(
        functools.partial(kernel, n_sub, n_freq, chunks),
        out_shape=(
            jax.ShapeDtypeStruct((columns, owned_cells), f32),
            jax.ShapeDtypeStruct((sub_here, modes), f32),
            jax.ShapeDtypeStruct((sub_here, modes, part), f32),
            jax.ShapeDtypeStruct((sub_here, kb), f32),
        ),
        in_specs=[hbm] * 11,
        out_specs=(vmem,) * 4,
        scratch_shapes=scratch,
        compiler_params=pltpu.CompilerParams(
            collective_id=0, has_side_effects=True, vmem_limit_bytes=48 * 1024 * 1024
        ),
    )(
        *(
            pltpu.with_memory_space_constraint(x, pltpu.HBM)
            for x in (
                freq_squared,
                incidence,
                block_count,
                mode_count,
                eigenvalues,
                flexibility,
                adjoint,
                displacement,
                stiffness,
                mass_matrix,
                coupling,
            )
        )
    )
    return pl.pallas_call(
        write_out,
        out_shape=tuple(jax.ShapeDtypeStruct(x.shape, x.dtype) for x in results),
        in_specs=[vmem] * 4,
        out_specs=(pl.BlockSpec(memory_space=pltpu.HBM),) * 4,
        scratch_shapes=[dma((4,))],
        compiler_params=pltpu.CompilerParams(vmem_limit_bytes=4 * 1024 * 1024),
    )(*results)


def solution(mesh):
    in_specs = (
        P("freq"),
        P("freq", "sub"),
        P("freq", "sub"),
        P("sub", None),
        P("sub"),
        P("sub"),
        P("sub", None, None),
        P("sub", None, None),
        P("sub", None, None),
        P("sub", None),
        P("sub", None),
    )
    out_specs = (P("freq", "sub"), P("sub", None), P("sub", None, "freq"), P("sub", None))
    body = functools.partial(shards, mesh.shape["sub"], mesh.shape["freq"])
    return jax.shard_map(body, mesh=mesh, in_specs=in_specs, out_specs=out_specs, check_vma=False)
```
